32 devices in a mesh: pairs: 2 (over y), blk: 8 (over z, x), panel: 2 (over core).
Axes of the slice: x: 2, y: 2, z: 4, core: 2. Of those that a mesh axis runs over, the one named last changes fastest.
Arguments:
- first_frame: bfloat16 [4096, 256], P(('pairs', 'blk', 'panel')), parts along dimension 0, may hold values from -8 to 8
- second_frame: bfloat16 [16, 8, 16, 256], P(('pairs', 'blk'), None, 'panel'), parts along dimension 0, may hold values from -8 to 8
Outputs:
- matched: float32 [4, 2, 4096], P(None, None, ('pairs', 'blk', 'panel')), parts along dimension 2
- energy: float32 [4, 4096], P(None, ('pairs', 'blk', 'panel')), parts along dimension 1
The draws below stay inside these ranges and needn't reach their ends.
There are 2 independent parts, one for each index of `pairs`. The reference program is written for one: setup_inputs(seed, part) draws one part's arguments, and reference() takes and returns one part's arrays. A program takes and returns all parts, laid end to end along the dimension named above; each array names one. Nothing has to cross between parts.
All inputs are finite; a program needn't handle non-finite values.
Results may differ from the reference program's by a relative error of at most 0.014.
Values may be sent and summed in bfloat16 or wider, within the bound.
A program may use at most 128 MiB of HBM per device.

```python
import math
import jax
import jax.numpy as jnp
from jax import lax

C = 256
LEVELS = 4
COLBLK = 8
BCOLS = 16
BAND = 8
KEYBLK = 8
H2 = 8
W2 = 128
Q = 2048


def draw_first_frame(key, part):
    noise_key = jax.random.fold_in(jax.random.fold_in(key, 11), 0)
    values = jax.random.truncated_normal(noise_key, -4.0, 4.0, (Q, C), jnp.float32)
    return values.astype(jnp.bfloat16)


def draw_second_frame(key, part):
    noise_key = jax.random.fold_in(jax.random.fold_in(key, 23), 0)
    shape = (KEYBLK, BAND, BCOLS, C)
    values = jax.random.truncated_normal(noise_key, -4.0, 4.0, shape, jnp.float32)
    return values.astype(jnp.bfloat16)


def setup_inputs(seed: int = 0, part: int = 0) -> dict:
    seeds = jax.random.split(jax.random.key(seed), 3)
    part_splits = jax.random.split(jax.random.fold_in(seeds[2], part), 3)
    first_frame = draw_first_frame(jax.random.fold_in(jax.random.fold_in(seeds[2], part), 71), part)
    second_frame = draw_second_frame(jax.random.fold_in(jax.random.fold_in(seeds[2], part), 71), part)
    return {"first_frame": first_frame, "second_frame": second_frame}


def grid_of(second_frame):
    row_blocks = KEYBLK // COLBLK
    blocked = second_frame.reshape(row_blocks, COLBLK, BAND, BCOLS, C)
    return jnp.transpose(blocked, (0, 2, 1, 3, 4)).reshape(H2, W2, C)

def build_levels(grid):
    result = [grid]
    pooled = grid.astype(jnp.float32)
    for level_index in range(1, LEVELS):
        rows_now, cols_now, channels = pooled.shape
        pooled = pooled.reshape(rows_now // 2, 2, cols_now // 2, 2, channels).mean(axis=(1, 3))
        result.append(pooled.astype(jnp.bfloat16))
    return result

def position_table(row_count, col_count, level_index):
    row_grid = jnp.broadcast_to(jnp.arange(row_count, dtype=jnp.float32)[:, None], (row_count, col_count))
    col_grid = jnp.broadcast_to(jnp.arange(col_count, dtype=jnp.float32)[None, :], (row_count, col_count))
    spacing = 2.0 ** level_index
    row_pos = (row_grid + 0.5) * (spacing / H2)
    col_pos = (col_grid + 0.5) * (spacing / W2)
    unit_row = jnp.ones_like(row_pos)
    return jnp.stack([unit_row.reshape(-1), row_pos.reshape(-1), col_pos.reshape(-1)])

def reference(first_frame, second_frame):
    levels = build_levels(grid_of(second_frame))
    block_rows = math.gcd(Q, 1024)
    query_blocks = first_frame.reshape(Q // block_rows, block_rows, C)
    energies = []
    matches = []
    for level_index in range(LEVELS):
        level_grid = levels[level_index]
        row_count = level_grid.shape[0]
        col_count = level_grid.shape[1]
        key_rows = level_grid.reshape(row_count * col_count, C)
        table = position_table(row_count, col_count, level_index)
        factor = 3.0 * 2.0 ** level_index / math.sqrt(C)

        def per_block(queries, key_rows=key_rows, table=table, factor=factor):
            scores = jnp.dot(queries, key_rows.T, preferred_element_type=jnp.float32) * factor
            maxima = lax.optimization_barrier(jnp.max(scores, axis=1))
            weights = jnp.exp(scores - maxima[:, None])
            totals = jnp.dot(table, weights.T, precision=lax.Precision.HIGHEST, preferred_element_type=jnp.float32)
            return (maxima, totals)
        maxima, totals = lax.map(per_block, query_blocks)
        maxima = maxima.reshape(Q)
        totals = jnp.transpose(totals, (1, 0, 2)).reshape(3, Q)
        energies.append(maxima + jnp.log(totals[0]))
        matches.append(totals[1:] / totals[0:1])
    return (jnp.stack(matches), jnp.stack(energies))
```

```python
import functools
import math

import jax
import jax.numpy as jnp
from jax import lax
from jax.experimental import pallas as pl
from jax.experimental.pallas import tpu as pltpu
from jax.sharding import PartitionSpec as P

LEVELS = 4
COLBLK = 8
BCOLS = 16
NEG = -1e30
MESH = pl.DeviceIdType.MESH


def inner_size(blk):
    inner = 1
    while blk % (inner * 2) == 0 and (inner * 2) ** 2 * 2 <= blk:
        inner *= 2
    return inner


def partials(scores, sources, rows, cols, total_rows, total_cols):
    n = len(sources)
    q = scores.shape[-1]
    col = lax.broadcasted_iota(jnp.int32, (cols, q), 0)
    tops, totals, row_sums, col_sums = [], [], [], []
    pooled = scores.reshape(n, rows, cols, q)
    for level in range(LEVELS):
        step = 2**level
        if level:
            height = rows // step
            pairs = pooled.reshape(n, height, 2, cols, q)
            pooled = pairs[:, :, 0] + pairs[:, :, 1]
            pooled = pooled + pltpu.roll(pooled, step // 2, 2)
            pooled = 0.5 * pooled
            valid = (col & (step - 1)) == step - 1
            values = jnp.where(valid[None, None], pooled, NEG)
        else:
            height = rows
            values = pooled
        top = jnp.max(jnp.max(values, axis=(0, 1)), axis=0, keepdims=True)
        weights = jnp.exp(values - top)
        col_in = ((col >> level).astype(jnp.float32) + 0.5) * (step / total_cols)
        total = row_sum = col_sum = None
        for s, (row_base, col_base) in enumerate(sources):
            part = weights[s, 0]
            part_row = weights[s, 0] * (0.5 * step / total_rows)
            for i in range(1, height):
                part = part + weights[s, i]
                part_row = part_row + weights[s, i] * ((i + 0.5) * step / total_rows)
            part_row = part_row + part * row_base
            part_col = part * (col_in + col_base)
            total = part if total is None else total + part
            row_sum = part_row if row_sum is None else row_sum + part_row
            col_sum = part_col if col_sum is None else col_sum + part_col
        tops.append(top)
        totals.append(jnp.sum(total, axis=0, keepdims=True))
        row_sums.append(jnp.sum(row_sum, axis=0, keepdims=True))
        col_sums.append(jnp.sum(col_sum, axis=0, keepdims=True))
    return tops + totals + row_sums + col_sums


def kernel(dims, q_ref, k_ref, matched_ref, energy_ref, qbuf, kbuf, sent, got, local_sem,
           k_send, k_recv, q_send, q_recv, p_send, p_recv):
    blk, panels, inner, rows, cols = dims
    outer, group = blk // inner, inner * panels
    keys = rows * cols
    total_rows, total_cols = rows * blk // COLBLK, BCOLS * COLBLK
    me_blk, me_panel = lax.axis_index("blk"), lax.axis_index("panel")
    me_outer, me_inner = me_blk // inner, me_blk % inner
    me_group = me_inner * panels + me_panel

    def line_id(shift):
        there = lax.rem(me_outer + shift + outer, outer)
        return {"blk": there * inner + me_inner, "panel": me_panel}

    def group_id(shift):
        there = lax.rem(me_group + shift + group, group)
        return {"blk": me_outer * inner + there // panels, "panel": there % panels}

    barrier = pltpu.get_barrier_semaphore()
    for d in range(1, outer):
        pl.semaphore_signal(barrier, inc=1, device_id=line_id(d), device_id_type=MESH)
    for d in range(1, group):
        pl.semaphore_signal(barrier, inc=1, device_id=group_id(d), device_id_type=MESH)
    own_k = pltpu.make_async_copy(k_ref, kbuf.at[0], local_sem.at[0])
    own_q = pltpu.make_async_copy(q_ref, qbuf.at[0], local_sem.at[1])
    own_k.start()
    own_q.start()
    own_k.wait()
    own_q.wait()
    pl.semaphore_wait(barrier, outer + group - 2)

    key_copies, query_copies = {}, {}
    for d in range(1, outer):
        key_copies[d] = pltpu.make_async_remote_copy(
            kbuf.at[0], kbuf.at[d], k_send.at[d - 1], k_recv.at[d - 1],
            device_id=line_id(d), device_id_type=MESH)
        key_copies[d].start()
    for d in range(1, group):
        query_copies[d] = pltpu.make_async_remote_copy(
            qbuf.at[0], qbuf.at[d], q_send.at[d - 1], q_recv.at[d - 1],
            device_id=group_id(d), device_id_type=MESH)
        query_copies[d].start()

    sources = []
    for d in range(outer):
        block = lax.rem(me_outer - d + outer, outer) * inner + me_inner
        row_base = (block // COLBLK).astype(jnp.float32) * (rows / total_rows)
        col_base = ((block % COLBLK) * BCOLS + me_panel * cols).astype(jnp.float32) * (1.0 / total_cols)
        sources.append((row_base, col_base))

    for d in range(1, outer):
        key_copies[d].wait_recv()
    all_keys = kbuf[...].reshape(outer * keys, kbuf.shape[-1])
    factor = 3.0 / math.sqrt(kbuf.shape[-1])

    def score(d):
        raw = lax.dot_general(all_keys, qbuf[d], (((1,), (1,)), ((), ())),
                              preferred_element_type=jnp.float32)
        rows_out = partials(raw * factor, sources, rows, cols, total_rows, total_cols)
        sent[d] = jnp.concatenate(rows_out, axis=0)

    back = {}
    for d in range(1, group):
        query_copies[d].wait_recv()
        score(d)
        back[d] = pltpu.make_async_remote_copy(
            sent.at[d], got.at[d], p_send.at[d - 1], p_recv.at[d - 1],
            device_id=group_id(-d), device_id_type=MESH)
        back[d].start()
    score(0)
    parts = [sent[0]]
    for d in range(1, group):
        back[d].wait_recv()
        parts.append(got[d])
    top = functools.reduce(jnp.maximum, [p[:LEVELS] for p in parts])
    sums = None
    for p in parts:
        scale = jnp.exp(p[:LEVELS] - top)
        term = [p[LEVELS * i : LEVELS * (i + 1)] * scale for i in (1, 2, 3)]
        sums = term if sums is None else [a + b for a, b in zip(sums, term)]
    total, row_sum, col_sum = sums
    energy_ref[...] = top + jnp.log(total)
    matched_ref[:, 0, :] = row_sum / total
    matched_ref[:, 1, :] = col_sum / total
    for copies in (key_copies, query_copies, back):
        for copy in copies.values():
            copy.wait_send()


def body(blk, panels, first_frame, second_frame):
    queries, channels = first_frame.shape
    _, rows, cols, _ = second_frame.shape
    inner = inner_size(blk)
    outer, group = blk // inner, inner * panels
    keys = second_frame.reshape(rows * cols, channels)
    dma = pltpu.SemaphoreType.DMA
    matched, energy = pl.pallas_call(
        functools.partial(kernel, (blk, panels, inner, rows, cols)),
        out_shape=(jax.ShapeDtypeStruct((LEVELS, 2, queries), jnp.float32),
                   jax.ShapeDtypeStruct((LEVELS, queries), jnp.float32)),
        in_specs=[pl.BlockSpec(memory_space=pl.ANY)] * 2,
        out_specs=(pl.BlockSpec(memory_space=pltpu.VMEM), pl.BlockSpec(memory_space=pltpu.VMEM)),
        scratch_shapes=[
            pltpu.VMEM((group, queries, channels), jnp.bfloat16),
            pltpu.VMEM((outer, rows * cols, channels), jnp.bfloat16),
            pltpu.VMEM((group, 4 * LEVELS, queries), jnp.float32),
            pltpu.VMEM((group, 4 * LEVELS, queries), jnp.float32),
            dma((2,)),
            dma((outer - 1,)), dma((outer - 1,)),
            dma((group - 1,)), dma((group - 1,)),
            dma((group - 1,)), dma((group - 1,)),
        ],
        compiler_params=pltpu.CompilerParams(collective_id=0, has_side_effects=True),
        name="corr",
    )(first_frame, keys)
    return matched, energy


def solution(mesh):
    placed = (P(("pairs", "blk", "panel"), None), P(("pairs", "blk"), None, "panel", None))
    return jax.shard_map(
        functools.partial(body, mesh.shape["blk"], mesh.shape["panel"]),
        mesh=mesh,
        in_specs=placed,
        out_specs=(P(None, None, ("pairs", "blk", "panel")), P(None, ("pairs", "blk", "panel"))),
        check_vma=False,
    )
```

```python
import functools
import math

import jax
import jax.numpy as jnp
from jax import lax
from jax.experimental import pallas as pl
from jax.experimental.pallas import tpu as pltpu
from jax.sharding import PartitionSpec as P

LEVELS = 4
COLBLK = 8
BCOLS = 16
NEG = -1e30
MESH = pl.DeviceIdType.MESH


def inner_size(blk):
    inner = 1
    while blk % (inner * 2) == 0 and (inner * 2) ** 2 * 2 <= blk:
        inner *= 2
    return inner


def partials(scores, sources, rows, cols, total_rows, total_cols):
    n = len(sources)
    q = scores.shape[-1]
    col = lax.broadcasted_iota(jnp.int32, (cols, q), 0)
    tops, totals, row_sums, col_sums = [], [], [], []
    pooled = scores.reshape(n, rows, cols, q)
    for level in range(LEVELS):
        step = 2**level
        if level:
            height = rows // step
            pairs = pooled.reshape(n, height, 2, cols, q)
            pooled = pairs[:, :, 0] + pairs[:, :, 1]
            pooled = pooled + pltpu.roll(pooled, step // 2, 2)
            pooled = 0.5 * pooled
            valid = (col & (step - 1)) == step - 1
            values = jnp.where(valid[None, None], pooled, NEG)
        else:
            height = rows
            values = pooled
        top = jnp.max(jnp.max(values, axis=(0, 1)), axis=0, keepdims=True)
        weights = jnp.exp(values - top)
        col_in = ((col >> level).astype(jnp.float32) + 0.5) * (step / total_cols)
        total = row_sum = col_sum = None
        for s, (row_base, col_base) in enumerate(sources):
            part = weights[s, 0]
            part_row = weights[s, 0] * (0.5 * step / total_rows)
            for i in range(1, height):
                part = part + weights[s, i]
                part_row = part_row + weights[s, i] * ((i + 0.5) * step / total_rows)
            part_row = part_row + part * row_base
            part_col = part * (col_in + col_base)
            total = part if total is None else total + part
            row_sum = part_row if row_sum is None else row_sum + part_row
            col_sum = part_col if col_sum is None else col_sum + part_col
        tops.append(top)
        totals.append(jnp.sum(total, axis=0, keepdims=True))
        row_sums.append(jnp.sum(row_sum, axis=0, keepdims=True))
        col_sums.append(jnp.sum(col_sum, axis=0, keepdims=True))
    return tops + totals + row_sums + col_sums


def kernel(dims, q_ref, k_ref, merged_ref, qbuf, kbuf, sent, got, local_sem,
           k_send, k_recv, q_send, q_recv, p_send, p_recv):
    blk, panels, inner, rows, cols = dims
    outer, group = blk // inner, inner * panels
    keys = rows * cols
    total_rows, total_cols = rows * blk // COLBLK, BCOLS * COLBLK
    me_blk, me_panel = lax.axis_index("blk"), lax.axis_index("panel")
    me_outer, me_inner = me_blk // inner, me_blk % inner
    me_group = me_inner * panels + me_panel

    def line_id(shift):
        there = lax.rem(me_outer + shift + outer, outer)
        return {"blk": there * inner + me_inner, "panel": me_panel}

    def group_id(shift):
        there = lax.rem(me_group + shift + group, group)
        return {"blk": me_outer * inner + there // panels, "panel": there % panels}

    barrier = pltpu.get_barrier_semaphore()
    for d in range(1, outer):
        pl.semaphore_signal(barrier, inc=1, device_id=line_id(d), device_id_type=MESH)
    for d in range(1, group):
        pl.semaphore_signal(barrier, inc=1, device_id=group_id(d), device_id_type=MESH)
    own_k = pltpu.make_async_copy(k_ref, kbuf.at[0], local_sem.at[0])
    own_q = pltpu.make_async_copy(q_ref, qbuf.at[0], local_sem.at[1])
    own_k.start()
    own_q.start()
    own_k.wait()
    own_q.wait()
    pl.semaphore_wait(barrier, outer + group - 2)

    key_copies, query_copies = {}, {}
    for d in range(1, outer):
        key_copies[d] = pltpu.make_async_remote_copy(
            kbuf.at[0], kbuf.at[d], k_send.at[d - 1], k_recv.at[d - 1],
            device_id=line_id(d), device_id_type=MESH)
        key_copies[d].start()
    for d in range(1, group):
        query_copies[d] = pltpu.make_async_remote_copy(
            qbuf.at[0], qbuf.at[d], q_send.at[d - 1], q_recv.at[d - 1],
            device_id=group_id(d), device_id_type=MESH)
        query_copies[d].start()

    sources = []
    for d in range(outer):
        block = lax.rem(me_outer - d + outer, outer) * inner + me_inner
        row_base = (block // COLBLK).astype(jnp.float32) * (rows / total_rows)
        col_base = ((block % COLBLK) * BCOLS + me_panel * cols).astype(jnp.float32) * (1.0 / total_cols)
        sources.append((row_base, col_base))

    for d in range(1, outer):
        key_copies[d].wait_recv()
    all_keys = kbuf[...].reshape(outer * keys, kbuf.shape[-1])
    factor = 3.0 / math.sqrt(kbuf.shape[-1])

    def score(d):
        raw = lax.dot_general(all_keys, qbuf[d], (((1,), (1,)), ((), ())),
                              preferred_element_type=jnp.float32)
        rows_out = partials(raw * factor, sources, rows, cols, total_rows, total_cols)
        sent[d] = jnp.concatenate(rows_out, axis=0)

    back = {}
    for d in range(1, group):
        query_copies[d].wait_recv()
        score(d)
        back[d] = pltpu.make_async_remote_copy(
            sent.at[d], got.at[d], p_send.at[d - 1], p_recv.at[d - 1],
            device_id=group_id(-d), device_id_type=MESH)
        back[d].start()
    score(0)
    parts = [sent[0]]
    for d in range(1, group):
        back[d].wait_recv()
        parts.append(got[d])
    top = functools.reduce(jnp.maximum, [p[:LEVELS] for p in parts])
    sums = None
    for p in parts:
        scale = jnp.exp(p[:LEVELS] - top)
        term = [p[LEVELS * i : LEVELS * (i + 1)] * scale for i in (1, 2, 3)]
        sums = term if sums is None else [a + b for a, b in zip(sums, term)]
    total, row_sum, col_sum = sums
    merged_ref[...] = jnp.concatenate([top, total, row_sum, col_sum], axis=0)
    for copies in (key_copies, query_copies, back):
        for copy in copies.values():
            copy.wait_send()


def finish(merged_ref, matched_ref, energy_ref):
    top, total = merged_ref[:LEVELS], merged_ref[LEVELS : 2 * LEVELS]
    energy_ref[...] = top + jnp.log(total)
    matched_ref[:, 0, :] = merged_ref[2 * LEVELS : 3 * LEVELS] / total
    matched_ref[:, 1, :] = merged_ref[3 * LEVELS :] / total


def body(blk, panels, first_frame, second_frame):
    queries, channels = first_frame.shape
    _, rows, cols, _ = second_frame.shape
    inner = inner_size(blk)
    outer, group = blk // inner, inner * panels
    keys = second_frame.reshape(rows * cols, channels)
    dma = pltpu.SemaphoreType.DMA
    merged = pl.pallas_call(
        functools.partial(kernel, (blk, panels, inner, rows, cols)),
        out_shape=jax.ShapeDtypeStruct((4 * LEVELS, queries), jnp.float32),
        in_specs=[pl.BlockSpec(memory_space=pl.ANY)] * 2,
        out_specs=pl.BlockSpec(memory_space=pltpu.VMEM),
        scratch_shapes=[
            pltpu.VMEM((group, queries, channels), jnp.bfloat16),
            pltpu.VMEM((outer, rows * cols, channels), jnp.bfloat16),
            pltpu.VMEM((group, 4 * LEVELS, queries), jnp.float32),
            pltpu.VMEM((group, 4 * LEVELS, queries), jnp.float32),
            dma((2,)),
            dma((outer - 1,)), dma((outer - 1,)),
            dma((group - 1,)), dma((group - 1,)),
            dma((group - 1,)), dma((group - 1,)),
        ],
        compiler_params=pltpu.CompilerParams(collective_id=0, has_side_effects=True),
        name="corr",
    )(first_frame, keys)
    return pl.pallas_call(
        finish,
        out_shape=(jax.ShapeDtypeStruct((LEVELS, 2, queries), jnp.float32),
                   jax.ShapeDtypeStruct((LEVELS, queries), jnp.float32)),
        in_specs=[pl.BlockSpec(memory_space=pltpu.VMEM)],
        out_specs=(pl.BlockSpec(memory_space=pltpu.VMEM), pl.BlockSpec(memory_space=pltpu.VMEM)),
        name="finish",
    )(merged)


def solution(mesh):
    placed = (P(("pairs", "blk", "panel"), None), P(("pairs", "blk"), None, "panel", None))
    return jax.shard_map(
        functools.partial(body, mesh.shape["blk"], mesh.shape["panel"]),
        mesh=mesh,
        in_specs=placed,
        out_specs=(P(None, None, ("pairs", "blk", "panel")), P(None, ("pairs", "blk", "panel"))),
        check_vma=False,
    )
```

```python
import functools
import math

import jax
import jax.numpy as jnp
from jax import lax
from jax.experimental import pallas as pl
from jax.experimental.pallas import tpu as pltpu
from jax.sharding import PartitionSpec as P

LEVELS = 4
COLBLK = 8
BCOLS = 16
NEG = -1e30
MESH = pl.DeviceIdType.MESH


def inner_size(blk):
    inner = 1
    while blk % (inner * 2) == 0 and (inner * 2) ** 2 * 2 <= blk:
        inner *= 2
    return inner


def partials(scores, sources, rows, cols, total_rows, total_cols):
    n = len(sources)
    q = scores.shape[-1]
    col = lax.broadcasted_iota(jnp.int32, (cols, q), 0)
    tops, totals, row_sums, col_sums = [], [], [], []
    pooled = scores.reshape(n, rows, cols, q)
    for level in range(LEVELS):
        step = 2**level
        if level:
            height = rows // step
            pairs = pooled.reshape(n, height, 2, cols, q)
            pooled = pairs[:, :, 0] + pairs[:, :, 1]
            pooled = pooled + pltpu.roll(pooled, step // 2, 2)
            pooled = 0.5 * pooled
            valid = (col & (step - 1)) == step - 1
            values = jnp.where(valid[None, None], pooled, NEG)
        else:
            height = rows
            values = pooled
        top = jnp.max(jnp.max(values, axis=(0, 1)), axis=0, keepdims=True)
        weights = jnp.exp(values - top)
        col_in = ((col >> level).astype(jnp.float32) + 0.5) * (step / total_cols)
        total = row_sum = col_sum = None
        for s, (row_base, col_base) in enumerate(sources):
            part = weights[s, 0]
            part_row = weights[s, 0] * (0.5 * step / total_rows)
            for i in range(1, height):
                part = part + weights[s, i]
                part_row = part_row + weights[s, i] * ((i + 0.5) * step / total_rows)
            part_row = part_row + part * row_base
            part_col = part * (col_in + col_base)
            total = part if total is None else total + part
            row_sum = part_row if row_sum is None else row_sum + part_row
            col_sum = part_col if col_sum is None else col_sum + part_col
        tops.append(top)
        totals.append(jnp.sum(total, axis=0, keepdims=True))
        row_sums.append(jnp.sum(row_sum, axis=0, keepdims=True))
        col_sums.append(jnp.sum(col_sum, axis=0, keepdims=True))
    return tops + totals + row_sums + col_sums


def kernel(dims, q_ref, k_ref, merged_ref, qbuf, kbuf, sent, got, local_sem,
           k_send, k_recv, q_send, q_recv, p_send, p_recv):
    blk, panels, inner, rows, cols = dims
    outer, group = blk // inner, inner * panels
    keys = rows * cols
    total_rows, total_cols = rows * blk // COLBLK, BCOLS * COLBLK
    me_blk, me_panel = lax.axis_index("blk"), lax.axis_index("panel")
    me_outer, me_inner = me_blk // inner, me_blk % inner
    me_group = me_inner * panels + me_panel

    def line_id(shift):
        there = lax.rem(me_outer + shift + outer, outer)
        return {"blk": there * inner + me_inner, "panel": me_panel}

    def group_id(shift):
        there = lax.rem(me_group + shift + group, group)
        return {"blk": me_outer * inner + there // panels, "panel": there % panels}

    barrier = pltpu.get_barrier_semaphore()
    for d in range(1, outer):
        pl.semaphore_signal(barrier, inc=1, device_id=line_id(d), device_id_type=MESH)
    for d in range(1, group):
        pl.semaphore_signal(barrier, inc=1, device_id=group_id(d), device_id_type=MESH)
    own_k = pltpu.make_async_copy(k_ref, kbuf.at[0], local_sem.at[0])
    own_q = pltpu.make_async_copy(q_ref, qbuf.at[0], local_sem.at[1])
    own_k.start()
    own_q.start()
    own_k.wait()
    own_q.wait()
    pl.semaphore_wait(barrier, outer + group - 2)

    key_copies, query_copies = {}, {}
    for d in range(1, outer):
        key_copies[d] = pltpu.make_async_remote_copy(
            kbuf.at[0], kbuf.at[d], k_send.at[d - 1], k_recv.at[d - 1],
            device_id=line_id(d), device_id_type=MESH)
        key_copies[d].start()
    for d in range(1, group):
        query_copies[d] = pltpu.make_async_remote_copy(
            qbuf.at[0], qbuf.at[d], q_send.at[d - 1], q_recv.at[d - 1],
            device_id=group_id(d), device_id_type=MESH)
        query_copies[d].start()

    sources = []
    for d in range(outer):
        block = lax.rem(me_outer - d + outer, outer) * inner + me_inner
        row_base = (block // COLBLK).astype(jnp.float32) * (rows / total_rows)
        col_base = ((block % COLBLK) * BCOLS + me_panel * cols).astype(jnp.float32) * (1.0 / total_cols)
        sources.append((row_base, col_base))

    for d in range(1, outer):
        key_copies[d].wait_recv()
    all_keys = kbuf[...].reshape(outer * keys, kbuf.shape[-1])
    factor = 3.0 / math.sqrt(kbuf.shape[-1])

    def score(d):
        raw = lax.dot_general(all_keys, qbuf[d], (((1,), (1,)), ((), ())),
                              preferred_element_type=jnp.float32)
        rows_out = partials(raw * factor, sources, rows, cols, total_rows, total_cols)
        sent[d] = jnp.concatenate(rows_out, axis=0)

    back = {}
    for d in range(1, group):
        query_copies[d].wait_recv()
        score(d)
        back[d] = pltpu.make_async_remote_copy(
            sent.at[d], got.at[d], p_send.at[d - 1], p_recv.at[d - 1],
            device_id=group_id(-d), device_id_type=MESH)
        back[d].start()
    score(0)
    parts = [sent[0]]
    for d in range(1, group):
        back[d].wait_recv()
        parts.append(got[d])
    top = functools.reduce(jnp.maximum, [p[:LEVELS] for p in parts])
    sums = None
    for p in parts:
        scale = jnp.exp(p[:LEVELS] - top)
        term = [p[LEVELS * i : LEVELS * (i + 1)] * scale for i in (1, 2, 3)]
        sums = term if sums is None else [a + b for a, b in zip(sums, term)]
    total, row_sum, col_sum = sums
    merged_ref[...] = jnp.concatenate([top, total, row_sum, col_sum], axis=0)
    for copies in (key_copies, query_copies, back):
        for copy in copies.values():
            copy.wait_send()


def finish(merged_ref, matched_ref, energy_ref):
    top, total = merged_ref[:LEVELS], merged_ref[LEVELS : 2 * LEVELS]
    energy_ref[...] = top + jnp.log(total)
    matched_ref[:, 0, :] = merged_ref[2 * LEVELS : 3 * LEVELS] / total
    matched_ref[:, 1, :] = merged_ref[3 * LEVELS :] / total


def body(blk, panels, first_frame, second_frame):
    queries, channels = first_frame.shape
    _, rows, cols, _ = second_frame.shape
    inner = inner_size(blk)
    outer, group = blk // inner, inner * panels
    keys = second_frame.reshape(rows * cols, channels)
    dma = pltpu.SemaphoreType.DMA
    merged = pl.pallas_call(
        functools.partial(kernel, (blk, panels, inner, rows, cols)),
        out_shape=pltpu.VMEM((4 * LEVELS, queries), jnp.float32),
        in_specs=[pl.BlockSpec(memory_space=pl.ANY)] * 2,
        out_specs=pl.BlockSpec(memory_space=pltpu.VMEM),
        scratch_shapes=[
            pltpu.VMEM((group, queries, channels), jnp.bfloat16),
            pltpu.VMEM((outer, rows * cols, channels), jnp.bfloat16),
            pltpu.VMEM((group, 4 * LEVELS, queries), jnp.float32),
            pltpu.VMEM((group, 4 * LEVELS, queries), jnp.float32),
            dma((2,)),
            dma((outer - 1,)), dma((outer - 1,)),
            dma((group - 1,)), dma((group - 1,)),
            dma((group - 1,)), dma((group - 1,)),
        ],
        compiler_params=pltpu.CompilerParams(collective_id=0, has_side_effects=True),
        name="corr",
    )(first_frame, keys)
    return pl.pallas_call(
        finish,
        out_shape=(jax.ShapeDtypeStruct((LEVELS, 2, queries), jnp.float32),
                   jax.ShapeDtypeStruct((LEVELS, queries), jnp.float32)),
        in_specs=[pl.BlockSpec(memory_space=pltpu.VMEM)],
        out_specs=(pl.BlockSpec(memory_space=pltpu.VMEM), pl.BlockSpec(memory_space=pltpu.VMEM)),
        name="finish",
    )(pltpu.with_memory_space_constraint(merged, pltpu.VMEM))


def solution(mesh):
    placed = (P(("pairs", "blk", "panel"), None), P(("pairs", "blk"), None, "panel", None))
    return jax.shard_map(
        functools.partial(body, mesh.shape["blk"], mesh.shape["panel"]),
        mesh=mesh,
        in_specs=placed,
        out_specs=(P(None, None, ("pairs", "blk", "panel")), P(None, ("pairs", "blk", "panel"))),
        check_vma=False,
    )
```

```python
import functools
import math

import jax
import jax.numpy as jnp
from jax import lax
from jax.experimental import pallas as pl
from jax.experimental.pallas import tpu as pltpu
from jax.sharding import PartitionSpec as P

LEVELS = 4
COLBLK = 8
BCOLS = 16
NEG = -1e30
MESH = pl.DeviceIdType.MESH


def inner_size(blk):
    inner = 1
    while blk % (inner * 2) == 0 and (inner * 2) ** 2 * 2 <= blk:
        inner *= 2
    return inner


def partials(scores, sources, rows, cols, total_rows, total_cols):
    n = len(sources)
    q = scores.shape[-1]
    col = lax.broadcasted_iota(jnp.int32, (cols, q), 0)
    tops, totals, row_sums, col_sums = [], [], [], []
    pooled = scores.reshape(n, rows, cols, q)
    for level in range(LEVELS):
        step = 2**level
        if level:
            height = rows // step
            pairs = pooled.reshape(n, height, 2, cols, q)
            pooled = pairs[:, :, 0] + pairs[:, :, 1]
            pooled = pooled + pltpu.roll(pooled, step // 2, 2)
            pooled = 0.5 * pooled
            valid = (col & (step - 1)) == step - 1
            values = jnp.where(valid[None, None], pooled, NEG)
        else:
            height = rows
            values = pooled
        top = jnp.max(jnp.max(values, axis=(0, 1)), axis=0, keepdims=True)
        weights = jnp.exp(values - top)
        col_in = ((col >> level).astype(jnp.float32) + 0.5) * (step / total_cols)
        total = row_sum = col_sum = None
        for s, (row_base, col_base) in enumerate(sources):
            part = weights[s, 0]
            part_row = weights[s, 0] * (0.5 * step / total_rows)
            for i in range(1, height):
                part = part + weights[s, i]
                part_row = part_row + weights[s, i] * ((i + 0.5) * step / total_rows)
            part_row = part_row + part * row_base
            part_col = part * (col_in + col_base)
            total = part if total is None else total + part
            row_sum = part_row if row_sum is None else row_sum + part_row
            col_sum = part_col if col_sum is None else col_sum + part_col
        tops.append(top)
        totals.append(jnp.sum(total, axis=0, keepdims=True))
        row_sums.append(jnp.sum(row_sum, axis=0, keepdims=True))
        col_sums.append(jnp.sum(col_sum, axis=0, keepdims=True))
    return tops + totals + row_sums + col_sums


def kernel(dims, q_ref, k_ref, merged_ref, qbuf, kbuf, sent, got, local_sem,
           k_send, k_recv, q_send, q_recv, p_send, p_recv):
    blk, panels, inner, rows, cols = dims
    outer, group = blk // inner, inner * panels
    keys = rows * cols
    total_rows, total_cols = rows * blk // COLBLK, BCOLS * COLBLK
    me_blk, me_panel = lax.axis_index("blk"), lax.axis_index("panel")
    me_outer, me_inner = me_blk // inner, me_blk % inner

    def line_id(shift):
        there = lax.rem(me_outer + shift + outer, outer)
        return {"blk": there * inner + me_inner, "panel": me_panel}

    def slot_id(slot, sign=1):
        there = lax.rem(me_inner + sign * (slot // panels) + inner, inner)
        side = lax.rem(me_panel + sign * (slot % panels) + panels, panels)
        return {"blk": me_outer * inner + there, "panel": side}

    barrier = pltpu.get_barrier_semaphore()
    for d in range(1, outer):
        pl.semaphore_signal(barrier, inc=1, device_id=line_id(d), device_id_type=MESH)
    for d in range(1, group):
        pl.semaphore_signal(barrier, inc=1, device_id=slot_id(d), device_id_type=MESH)
    own_k = pltpu.make_async_copy(k_ref, kbuf.at[0], local_sem.at[0])
    own_q = pltpu.make_async_copy(q_ref, qbuf.at[0], local_sem.at[1])
    own_k.start()
    own_q.start()
    own_k.wait()
    own_q.wait()
    pl.semaphore_wait(barrier, outer + group - 2)

    key_copies, query_copies = {}, {}
    for d in range(1, outer):
        key_copies[d] = pltpu.make_async_remote_copy(
            kbuf.at[0], kbuf.at[d], k_send.at[d - 1], k_recv.at[d - 1],
            device_id=line_id(d), device_id_type=MESH)
        key_copies[d].start()
    for d in range(1, group):
        query_copies[d] = pltpu.make_async_remote_copy(
            qbuf.at[0], qbuf.at[d], q_send.at[d - 1], q_recv.at[d - 1],
            device_id=slot_id(d), device_id_type=MESH)
        query_copies[d].start()

    sources = []
    for d in range(outer):
        block = lax.rem(me_outer - d + outer, outer) * inner + me_inner
        row_base = (block // COLBLK).astype(jnp.float32) * (rows / total_rows)
        col_base = ((block % COLBLK) * BCOLS + me_panel * cols).astype(jnp.float32) * (1.0 / total_cols)
        sources.append((row_base, col_base))

    for d in range(1, outer):
        key_copies[d].wait_recv()
    all_keys = kbuf[...].reshape(outer * keys, kbuf.shape[-1])
    factor = 3.0 / math.sqrt(kbuf.shape[-1])

    def score(d):
        raw = lax.dot_general(all_keys, qbuf[d], (((1,), (1,)), ((), ())),
                              preferred_element_type=jnp.float32)
        rows_out = partials(raw * factor, sources, rows, cols, total_rows, total_cols)
        sent[d] = jnp.concatenate(rows_out, axis=0)

    back = {}
    for d in sorted(range(1, group), key=lambda d: d < panels):
        query_copies[d].wait_recv()
        score(d)
        back[d] = pltpu.make_async_remote_copy(
            sent.at[d], got.at[d], p_send.at[d - 1], p_recv.at[d - 1],
            device_id=slot_id(d, -1), device_id_type=MESH)
        back[d].start()
    score(0)
    parts = [sent[0]]
    for d in range(1, group):
        back[d].wait_recv()
        parts.append(got[d])
    top = functools.reduce(jnp.maximum, [p[:LEVELS] for p in parts])
    sums = None
    for p in parts:
        scale = jnp.exp(p[:LEVELS] - top)
        term = [p[LEVELS * i : LEVELS * (i + 1)] * scale for i in (1, 2, 3)]
        sums = term if sums is None else [a + b for a, b in zip(sums, term)]
    total, row_sum, col_sum = sums
    merged_ref[...] = jnp.concatenate([top, total, row_sum, col_sum], axis=0)
    for copies in (key_copies, query_copies, back):
        for copy in copies.values():
            copy.wait_send()


def finish(merged_ref, matched_ref, energy_ref):
    top, total = merged_ref[:LEVELS], merged_ref[LEVELS : 2 * LEVELS]
    energy_ref[...] = top + jnp.log(total)
    matched_ref[:, 0, :] = merged_ref[2 * LEVELS : 3 * LEVELS] / total
    matched_ref[:, 1, :] = merged_ref[3 * LEVELS :] / total


def body(blk, panels, first_frame, second_frame):
    queries, channels = first_frame.shape
    _, rows, cols, _ = second_frame.shape
    inner = inner_size(blk)
    outer, group = blk // inner, inner * panels
    keys = second_frame.reshape(rows * cols, channels)
    dma = pltpu.SemaphoreType.DMA
    merged = pl.pallas_call(
        functools.partial(kernel, (blk, panels, inner, rows, cols)),
        out_shape=pltpu.VMEM((4 * LEVELS, queries), jnp.float32),
        in_specs=[pl.BlockSpec(memory_space=pl.ANY)] * 2,
        out_specs=pl.BlockSpec(memory_space=pltpu.VMEM),
        scratch_shapes=[
            pltpu.VMEM((group, queries, channels), jnp.bfloat16),
            pltpu.VMEM((outer, rows * cols, channels), jnp.bfloat16),
            pltpu.VMEM((group, 4 * LEVELS, queries), jnp.float32),
            pltpu.VMEM((group, 4 * LEVELS, queries), jnp.float32),
            dma((2,)),
            dma((outer - 1,)), dma((outer - 1,)),
            dma((group - 1,)), dma((group - 1,)),
            dma((group - 1,)), dma((group - 1,)),
        ],
        compiler_params=pltpu.CompilerParams(collective_id=0, has_side_effects=True),
        name="corr",
    )(first_frame, keys)
    return pl.pallas_call(
        finish,
        out_shape=(jax.ShapeDtypeStruct((LEVELS, 2, queries), jnp.float32),
                   jax.ShapeDtypeStruct((LEVELS, queries), jnp.float32)),
        in_specs=[pl.BlockSpec(memory_space=pltpu.VMEM)],
        out_specs=(pl.BlockSpec(memory_space=pltpu.VMEM), pl.BlockSpec(memory_space=pltpu.VMEM)),
        name="finish",
    )(pltpu.with_memory_space_constraint(merged, pltpu.VMEM))


def solution(mesh):
    placed = (P(("pairs", "blk", "panel"), None), P(("pairs", "blk"), None, "panel", None))
    return jax.shard_map(
        functools.partial(body, mesh.shape["blk"], mesh.shape["panel"]),
        mesh=mesh,
        in_specs=placed,
        out_specs=(P(None, None, ("pairs", "blk", "panel")), P(None, ("pairs", "blk", "panel"))),
        check_vma=False,
    )
```
